32 devices in a mesh: groups: 2 (over y), snap: 4 (over x, core), space: 4 (over z).
Axes of the slice: x: 2, y: 2, z: 4, core: 2. Of those that a mesh axis runs over, the one named last changes fastest.
Arguments:
- snapshots: bfloat16 [16384, 4096], P('space', ('groups', 'snap')), parts along dimension 1, may hold values from -12 to 12
- factor_blocks: bfloat16 [128, 4, 128, 128], P('space'), may hold values from -0.375 to 0.375
- factor_cols: int32 [128, 4], P('space'), may hold values from 0 to 31, as said below
- factor_counts: int32 [128], P('space'), may hold values from 1 to 4, as said below
- start_basis: float32 [4096, 128], P(('groups', 'snap')), parts along dimension 0, may hold values from -150 to 150
- merge_starts: float32 [3, 256, 128], replicated, may hold values from -150 to 150
Outputs:
- modes: bfloat16 [16384, 256], P(('space', 'snap'), 'groups'), parts along dimension 1
The draws below stay inside these ranges and needn't reach their ends.
There are 2 independent parts, one for each index of `groups`. The reference program is written for one: setup_inputs(seed, part) draws one part's arguments, and reference() takes and returns one part's arrays. A program takes and returns all parts, laid end to end along the dimension named above; an argument that names none is the same for every part. Nothing has to cross between parts.
Inputs may be any that keep to these rules, and one draw needn't show every extreme that they name: `factor_cols`: each entry names one of the 32 row blocks of the same group as its row block. `factor_counts`: slots at or after the count are not part of the factor.
All inputs are finite; a program needn't handle non-finite values.
Results may differ from the reference program's by a relative error of at most 0.011.
Values may be sent and summed in bfloat16 or wider, within the bound.
A program may use at most 128 MiB of HBM per device.

```python
import jax
import jax.numpy as jnp
from jax import lax

BS = 128
NNZ = 4
K = 128
RB_DEV = 32
S_DEV = 512
ROWS = 16384
NRB = 128
SNAPS = 2048
MERGES = 3
LEVELS = 2
N_SNAP = 4


def draw_factor_cols(key, part):
    others = jax.random.randint(key, (NRB, NNZ), 0, RB_DEV, dtype=jnp.int32)
    own_block = jnp.arange(NRB, dtype=jnp.int32) % RB_DEV
    return others.at[:, 0].set(own_block)


def draw_factor_counts(key, part):
    counts = jax.random.randint(key, (NRB,), 1, NNZ + 1, dtype=jnp.int32)
    return counts.at[0].set(NNZ).at[1].set(1)


def noise_field(key, shape):
    return jnp.clip(jax.random.normal(key, shape, jnp.float32), -6.0, 6.0)


def draw_snapshots(key, part):
    values = noise_field(jax.random.fold_in(key, 11), (ROWS, SNAPS))
    return values.astype(jnp.bfloat16)


def dominant_start(key, count, height, width):
    values = noise_field(key, (count, height, width))
    rows = jnp.arange(height, dtype=jnp.int32)[:, None]
    cols = jnp.arange(width, dtype=jnp.int32)[None, :]
    diagonal = (rows == cols).astype(jnp.float32) * (3.0 * jnp.sqrt(jnp.float32(height)))
    return values + diagonal[None]


def draw_start_basis(key, part):
    return dominant_start(jax.random.fold_in(key, 21), N_SNAP, S_DEV, K).reshape(SNAPS, K)


def draw_merge_starts(key, part):
    return dominant_start(jax.random.fold_in(key, 31), MERGES, 2 * K, K)


def shard_levels(stream_key, dims, cuts, least, high):
    loudness = 1.0
    for position, shards_of in cuts:
        steps = jax.random.uniform(jax.random.fold_in(jax.random.fold_in(stream_key, 6), position), (shards_of,), jnp.float32, least / len(cuts), high / len(cuts))
        loudness = loudness * jnp.repeat(jnp.exp(steps), dims[position] // shards_of).reshape((-1,) + (1,) * (len(dims) - 1 - position))
    return loudness


def centred(stream_key, dims, scale, bound, shards=(), kind=jnp.bfloat16):
    loudness = shard_levels(stream_key, dims, shards, -0.22, 0.18) if shards else 1.0
    array = jax.random.normal(stream_key, dims, jnp.float32) * scale * loudness
    return jnp.minimum(jnp.maximum(array, -bound), bound).astype(kind)


def setup_inputs(seed: int = 0, part: int = 0) -> dict:
    key_list = jax.random.split(jax.random.key(seed), 7)
    own_keys = jax.random.split(jax.random.fold_in(key_list[6], part), 7)
    snapshots = draw_snapshots(jax.random.fold_in(jax.random.fold_in(key_list[6], part), 71), part)
    factor_blocks = centred(key_list[1], (NRB, NNZ, BS, BS), (2 * BS) ** -0.5, 0.375, ((0, 4),))
    factor_cols = draw_factor_cols(jax.random.fold_in(key_list[6], 71), part)
    factor_counts = draw_factor_counts(jax.random.fold_in(key_list[6], 71), part)
    start_basis = draw_start_basis(jax.random.fold_in(jax.random.fold_in(key_list[6], part), 71), part)
    merge_starts = draw_merge_starts(jax.random.fold_in(key_list[6], 71), part)
    return dict(snapshots=snapshots, factor_blocks=factor_blocks, factor_cols=factor_cols, factor_counts=factor_counts, start_basis=start_basis, merge_starts=merge_starts)


HIGH = lax.Precision.HIGHEST

def orthonormal(matrix):
    cross_gram = jnp.dot(matrix.T, matrix, precision=HIGH)
    lower_factor = jnp.linalg.cholesky(cross_gram)
    return lax.linalg.triangular_solve(lower_factor, matrix, left_side=False, lower=True, transpose_a=True)

def weigh(group, factor_blocks, factor_cols, factor_counts):
    blocks_in = group.reshape(NRB, BS, S_DEV)
    base_block = jnp.arange(NRB, dtype=jnp.int32) // RB_DEV * RB_DEV
    accumulated = jnp.zeros((NRB, BS, S_DEV), jnp.float32)
    for slot_index in range(NNZ):
        live_mask = (slot_index < factor_counts).astype(jnp.float32)
        factor = factor_blocks[:, slot_index].astype(jnp.float32) * live_mask[:, None, None]
        source = jnp.take(blocks_in, (base_block + factor_cols[:, slot_index]).astype(jnp.int32), axis=0)
        accumulated = accumulated + jnp.einsum('bij,bjs->bis', factor, source.astype(jnp.float32))
    return accumulated.astype(jnp.bfloat16).reshape(ROWS, S_DEV)

def merge(left_node, right_node, start_vectors):
    paired = jnp.concatenate([left_node, right_node], axis=1)
    cross_gram = jnp.dot(paired.T.astype(jnp.float32), paired.astype(jnp.float32), preferred_element_type=jnp.float32)
    mixing = orthonormal(jnp.dot(cross_gram, start_vectors, precision=HIGH)).astype(jnp.bfloat16)
    return jnp.dot(paired.astype(jnp.float32), mixing.astype(jnp.float32), preferred_element_type=jnp.float32).astype(jnp.bfloat16)

def reference(snapshots, factor_blocks, factor_cols, factor_counts, start_basis, merge_starts):

    def compress(group_index):
        group = lax.dynamic_slice_in_dim(snapshots, group_index * S_DEV, S_DEV, 1)
        basis = lax.dynamic_slice_in_dim(start_basis, group_index * S_DEV, S_DEV, 0)
        weighted = weigh(group, factor_blocks, factor_cols, factor_counts)
        group_gram = jnp.dot(weighted.T.astype(jnp.float32), weighted.astype(jnp.float32), preferred_element_type=jnp.float32)
        for sweep_index in range(2):
            basis = orthonormal(jnp.dot(group_gram, basis, precision=HIGH))
        return jnp.dot(weighted.astype(jnp.float32), basis.astype(jnp.bfloat16).astype(jnp.float32), preferred_element_type=jnp.float32).astype(jnp.bfloat16)
    panels = lax.map(compress, jnp.arange(N_SNAP, dtype=jnp.int32))
    nodes = [panels[index] for index in range(N_SNAP)]
    offset_index = 0
    for level_index in range(LEVELS):
        pair_count = len(nodes) // 2
        nodes = [merge(nodes[2 * index], nodes[2 * index + 1], merge_starts[offset_index + index]) for index in range(pair_count)]
        offset_index = offset_index + pair_count
    return nodes[0]
```

```python
import functools

import jax
import jax.numpy as jnp
from jax import lax
from jax.experimental import pallas as pl
from jax.experimental.pallas import tpu as pltpu
from jax.sharding import PartitionSpec as P

HIGH = lax.Precision.HIGHEST
MESH = pl.DeviceIdType.MESH
F32 = jnp.float32
BF16 = jnp.bfloat16
VMEM = pl.BlockSpec(memory_space=pltpu.VMEM)
ROWS_IN_STEP = 8
TN = (((0,), (0,)), ((), ()))
NT = (((1,), (1,)), ((), ()))


def dot(a, b, dims=(((1,), (0,)), ((), ())), precision=None):
    return lax.dot_general(a, b, dims, precision=precision, preferred_element_type=F32)


def upper_blocks(count):
    return [(i, j) for i in range(count) for j in range(i, count)]


def weigh_kernel(cols_ref, counts_ref, snaps_ref, blocks_ref, weighted_ref, tri_ref, gram):
    step = pl.program_id(0)
    in_step, slots, width, _ = blocks_ref.shape
    for i in range(in_step):
        row = step * in_step + i
        count = counts_ref[row]
        factors = []
        sources = []
        for slot in range(slots):
            factor = blocks_ref[i, slot]
            factors.append(jnp.where(slot < count, factor, jnp.zeros_like(factor)))
            start = pl.multiple_of(cols_ref[row, slot] * width, width)
            sources.append(snaps_ref[pl.ds(start, width), :])
        product = dot(jnp.concatenate(factors, axis=1), jnp.concatenate(sources, axis=0))
        weighted_ref[i * width : (i + 1) * width, :] = product.astype(BF16)
    size = gram.shape[0]
    tall = 256

    @pl.when(step == 0)
    def _():
        gram[...] = jnp.zeros_like(gram)

    for low in range(0, size, tall):
        gram[low : low + tall, low:] += dot(
            weighted_ref[:, low : low + tall], weighted_ref[:, low:], TN
        )

    @pl.when(step == pl.num_programs(0) - 1)
    def _():
        for index, (i, j) in enumerate(upper_blocks(size // 128)):
            tri_ref[index] = gram[i * 128 : (i + 1) * 128, j * 128 : (j + 1) * 128]


def weigh(snapshots, factor_blocks, factor_cols, factor_counts):
    rows, size = snapshots.shape
    row_blocks, slots, width, _ = factor_blocks.shape
    in_step = ROWS_IN_STEP
    count = len(upper_blocks(size // 128))
    return pl.pallas_call(
        weigh_kernel,
        grid=(row_blocks // in_step,),
        in_specs=[
            pl.BlockSpec(memory_space=pltpu.SMEM),
            pl.BlockSpec(memory_space=pltpu.SMEM),
            pl.BlockSpec((rows, size), lambda s: (0, 0)),
            pl.BlockSpec((in_step, slots, width, width), lambda s: (s, 0, 0, 0)),
        ],
        out_specs=[
            pl.BlockSpec((in_step * width, size), lambda s: (s, 0)),
            pl.BlockSpec((count, 128, 128), lambda s: (0, 0, 0)),
        ],
        out_shape=[
            jax.ShapeDtypeStruct((rows, size), BF16),
            jax.ShapeDtypeStruct((count, 128, 128), F32),
        ],
        scratch_shapes=[pltpu.VMEM((size, size), F32)],
        name="weigh",
    )(factor_cols, factor_counts, snapshots, factor_blocks)


def line_kernel(n, own, total, pre_in, pre_out, suf_in, suf_out, sems):
    me = lax.axis_index("space")
    has_left = me > 0
    has_right = me < n - 1
    barrier = pltpu.get_barrier_semaphore()

    @pl.when(has_left)
    def _():
        pl.semaphore_signal(barrier, inc=1, device_id={"space": me - 1}, device_id_type=MESH)

    @pl.when(has_right)
    def _():
        pl.semaphore_signal(barrier, inc=1, device_id={"space": me + 1}, device_id_type=MESH)

    pl.semaphore_wait(barrier, has_left.astype(jnp.int32) + has_right.astype(jnp.int32))

    chunks = own.shape[0]

    def copy(kind, c, other):
        source, target = ((pre_out, pre_in), (suf_out, suf_in))[kind]
        return pltpu.make_async_remote_copy(
            src_ref=source.at[c],
            dst_ref=target.at[c],
            send_sem=sems.at[2 * kind, c],
            recv_sem=sems.at[2 * kind + 1, c],
            device_id={"space": other},
            device_id_type=MESH,
        )

    for c in range(chunks):
        for kind, has_from, has_to, to, out, arrived in (
            (0, has_left, has_right, me + 1, pre_out, pre_in),
            (1, has_right, has_left, me - 1, suf_out, suf_in),
        ):

            @pl.when(has_from)
            def _():
                copy(kind, c, me).wait_recv()

            @pl.when(jnp.logical_and(has_to, has_from))
            def _():
                out[c] = (own[c] + arrived[c].astype(F32)).astype(BF16)

            @pl.when(jnp.logical_and(has_to, jnp.logical_not(has_from)))
            def _():
                out[c] = own[c].astype(BF16)

            @pl.when(has_to)
            def _():
                copy(kind, c, to).start()

    for c in range(chunks):
        total[c] = own[c]

    @pl.when(has_left)
    def _():
        for c in range(chunks):
            total[c] += pre_in[c].astype(F32)

    @pl.when(has_right)
    def _():
        for c in range(chunks):
            total[c] += suf_in[c].astype(F32)

    for c in range(chunks):

        @pl.when(has_right)
        def _():
            copy(0, c, me).wait_send()

        @pl.when(has_left)
        def _():
            copy(1, c, me).wait_send()


def sum_over_space(blocks):
    n = lax.axis_size("space")
    return pl.pallas_call(
        functools.partial(line_kernel, n),
        in_specs=[VMEM],
        out_specs=VMEM,
        out_shape=jax.ShapeDtypeStruct(blocks.shape, F32),
        scratch_shapes=[pltpu.VMEM(blocks.shape, BF16)] * 4
        + [pltpu.SemaphoreType.DMA((4, blocks.shape[0]))],
        compiler_params=pltpu.CompilerParams(collective_id=0, has_side_effects=True),
        name="line_sum",
    )(blocks)


def eliminate(a, e, lane):
    a, e = list(a), list(e)
    groups = len(a)
    row = lax.broadcasted_iota(jnp.int32, (8, 128), 0)
    scale = [jnp.zeros((8, 128), F32)] * groups
    for g in range(groups):
        cols = {
            h: [
                jnp.broadcast_to(a[h][:, lane + 8 * g + k : lane + 8 * g + k + 1], (8, 128))
                for k in range(8)
            ]
            for h in range(g, groups)
        }
        for k in range(8):
            pivot = jnp.broadcast_to(cols[g][k][k : k + 1, :], (8, 128))
            inverse = 1.0 / pivot
            scale[g] = jnp.where(row == k, lax.rsqrt(pivot), scale[g])
            a_row = jnp.broadcast_to(a[g][k : k + 1, :], (8, 128))
            e_row = jnp.broadcast_to(e[g][k : k + 1, :], (8, 128))
            heads = {
                m: jnp.broadcast_to(cols[g][m][k : k + 1, :], (8, 128)) for m in range(k + 1, 8)
            }
            for h in range(g, groups):
                if h == g and k == 7:
                    continue
                f = cols[h][k] * inverse
                if h == g:
                    f = jnp.where(row > k, f, 0.0)
                for m in range(k + 1, 8):
                    cols[h][m] = cols[h][m] - f * heads[m]
                a[h] = a[h] - f * a_row
                e[h] = e[h] - f * e_row
    return [x * s for x, s in zip(a, scale)], [x * s for x, s in zip(e, scale)]


def inverse_factor(cross):
    size = cross.shape[0]
    row = lax.broadcasted_iota(jnp.int32, (size, size), 0)
    col = lax.broadcasted_iota(jnp.int32, (size, size), 1)
    both = jnp.concatenate([cross, (row == col).astype(F32)], axis=1)
    done = []
    for p in range(size // 32):
        rows = [both[p * 32 + 8 * g : p * 32 + 8 * g + 8] for g in range(4)]
        a, e = eliminate([r[:, :size] for r in rows], [r[:, size:] for r in rows], p * 32)
        a, e = jnp.concatenate(a, axis=0), jnp.concatenate(e, axis=0)
        done.append(e)
        if p < size // 32 - 1:
            both = both - dot(a, jnp.concatenate([a, e], axis=1), TN, HIGH)
    return jnp.concatenate(done, axis=0)


def orthonormal(z):
    return dot(z, inverse_factor(dot(z, z, TN, HIGH)), NT, HIGH)


def compress_kernel(tri_ref, start_ref, weighted_ref, panel_ref, diag_ref, gram, basis):
    size = gram.shape[0]
    for index, (i, j) in enumerate(upper_blocks(size // 128)):
        block = tri_ref[index]
        gram[i * 128 : (i + 1) * 128, j * 128 : (j + 1) * 128] = block
        if i != j:
            gram[j * 128 : (j + 1) * 128, i * 128 : (i + 1) * 128] = block.T
    basis[...] = start_ref[...]

    def sweep(_, carry):
        basis[...] = orthonormal(dot(gram[...], basis[...], precision=HIGH))
        return carry

    lax.fori_loop(0, 2, sweep, 0)
    rounded = basis[...].astype(BF16)
    tall = 1024
    for low in range(0, weighted_ref.shape[0], tall):
        panel_ref[low : low + tall, :] = dot(weighted_ref[low : low + tall, :], rounded).astype(BF16)
    wide = rounded.astype(F32)
    diag_ref[...] = dot(wide, dot(gram[...], wide, precision=HIGH), TN, HIGH)


def compress(tri, start_basis, weighted):
    size, modes = start_basis.shape
    return pl.pallas_call(
        compress_kernel,
        in_specs=[VMEM] * 3,
        out_specs=[VMEM] * 2,
        out_shape=[
            jax.ShapeDtypeStruct((weighted.shape[0], modes), BF16),
            jax.ShapeDtypeStruct((modes, modes), F32),
        ],
        scratch_shapes=[pltpu.VMEM((size, size), F32), pltpu.VMEM((size, modes), F32)],
        name="compress",
    )(tri, start_basis, weighted)


def flipped(index, bit):
    return index + (1 - 2 * (index // (1 << bit) % 2)) * (1 << bit)


def pair_kernel(
    n, level, panel, diag, pair, cross_gram, got, got_diag, out, came, z_out, z_came, sems, x_sems, z_sems
):
    snap = lax.axis_index("snap")
    space = lax.axis_index("space")
    bit = snap // (1 << level) % 2
    partner = flipped(snap, level)
    half, _, rows, modes = panel.shape
    barrier = pltpu.get_barrier_semaphore()
    for b in range(level + 1):
        pl.semaphore_signal(
            barrier, inc=1, device_id={"snap": flipped(snap, b)}, device_id_type=MESH
        )
    for k in range(1, n):
        pl.semaphore_signal(
            barrier, inc=1, device_id={"space": lax.rem(space + k, n)}, device_id_type=MESH
        )
    pl.semaphore_wait(barrier, level + n)

    def remote(source, target, send, recv, device):
        return pltpu.make_async_remote_copy(
            src_ref=source,
            dst_ref=target,
            send_sem=send,
            recv_sem=recv,
            device_id=device,
            device_id_type=MESH,
        )

    copies = [
        remote(panel.at[h, 1 - bit], got.at[h], sems.at[0, h], sems.at[1, h], {"snap": partner})
        for h in range(half)
    ]
    copies.append(
        remote(diag, got_diag, sems.at[0, half], sems.at[1, half], {"snap": partner})
    )
    for c in copies:
        c.start()
    cross = jnp.zeros((modes, modes), F32)
    upper = bit == 1
    for h in range(half):
        copies[h].wait_recv()
        mine, theirs = panel[h, bit], got[h]
        left = jnp.where(upper, theirs, mine)
        right = jnp.where(upper, mine, theirs)
        pair[h * rows : (h + 1) * rows, :modes] = left
        pair[h * rows : (h + 1) * rows, modes:] = right
        cross = cross + dot(left, right, TN)
    for b in range(level + 1):
        out[b] = cross
        step = remote(
            out.at[b], came.at[b], x_sems.at[0, b], x_sems.at[1, b], {"snap": flipped(snap, b)}
        )
        step.start()
        step.wait_recv()
        cross = cross + came[b]
        copies.append(step)
    z_out[...] = cross.astype(BF16)
    steps = [
        remote(
            z_out,
            z_came.at[k - 1],
            z_sems.at[0, k - 1],
            z_sems.at[1, k - 1],
            {"space": lax.rem(space + k, n)},
        )
        for k in range(1, n)
    ]
    for s in steps:
        s.start()
    copies[half].wait_recv()
    cross_gram[:modes, :modes] = jnp.where(upper, got_diag[...], diag[...])
    cross_gram[modes:, modes:] = jnp.where(upper, diag[...], got_diag[...])
    for k, s in enumerate(steps):
        s.wait_recv()
        cross = cross + z_came[k].astype(F32)
    cross_gram[:modes, modes:] = cross
    cross_gram[modes:, :modes] = cross.T
    for c in copies + steps:
        c.wait_send()


def pair_up(panel, diag, level, parts):
    n = lax.axis_size("space")
    rows, modes = panel.shape
    half = parts // 2
    rows_in = rows // parts
    return pl.pallas_call(
        functools.partial(pair_kernel, n, level),
        in_specs=[VMEM] * 2,
        out_specs=[VMEM] * 2,
        out_shape=[
            jax.ShapeDtypeStruct((rows // 2, 2 * modes), BF16),
            jax.ShapeDtypeStruct((2 * modes, 2 * modes), F32),
        ],
        scratch_shapes=[
            pltpu.VMEM((half, rows_in, modes), BF16),
            pltpu.VMEM((modes, modes), F32),
            pltpu.VMEM((level + 1, modes, modes), F32),
            pltpu.VMEM((level + 1, modes, modes), F32),
            pltpu.VMEM((modes, modes), BF16),
            pltpu.VMEM((n - 1, modes, modes), BF16),
            pltpu.SemaphoreType.DMA((2, half + 1)),
            pltpu.SemaphoreType.DMA((2, level + 1)),
            pltpu.SemaphoreType.DMA((2, n - 1)),
        ],
        compiler_params=pltpu.CompilerParams(collective_id=1 + level, has_side_effects=True),
        name="pair_up",
    )(panel.reshape(half, 2, rows_in, modes), diag)


def mix_kernel(snap_count, level, pair, cross_gram, starts, *outs):
    snap = lax.axis_index("snap")
    index = snap_count - (snap_count >> level) + snap // (1 << (level + 1))
    steered = dot(cross_gram[...], starts[index], precision=HIGH)
    mixing = orthonormal(steered).astype(BF16)
    outs[0][...] = dot(pair[...], mixing).astype(BF16)
    if len(outs) > 1:
        wide = mixing.astype(F32)
        outs[1][...] = dot(wide, dot(cross_gram[...], wide, precision=HIGH), TN, HIGH)


def mix(pair, cross_gram, merge_starts, level, snap_count, last):
    rows = pair.shape[0]
    modes = merge_starts.shape[2]
    shapes = [jax.ShapeDtypeStruct((rows, modes), BF16)]
    if not last:
        shapes.append(jax.ShapeDtypeStruct((modes, modes), F32))
    return pl.pallas_call(
        functools.partial(mix_kernel, snap_count, level),
        in_specs=[VMEM] * 3,
        out_specs=[VMEM] * len(shapes),
        out_shape=shapes,
        name="mix",
    )(pair, cross_gram, merge_starts)


def local(snapshots, factor_blocks, factor_cols, factor_counts, start_basis, merge_starts):
    weighted, tri = weigh(snapshots, factor_blocks, factor_cols, factor_counts)
    tri = sum_over_space(tri)
    panel, diag = compress(tri, start_basis, weighted)
    parts = lax.axis_size("snap")
    snap_count = parts
    levels = snap_count.bit_length() - 1
    for level in range(levels):
        pair, cross_gram = pair_up(panel, diag, level, parts)
        parts //= 2
        last = level == levels - 1
        made = mix(pair, cross_gram, merge_starts, level, snap_count, last)
        panel = made[0]
        diag = None if last else made[1]
    return panel


def solution(mesh):
    return jax.shard_map(
        local,
        mesh=mesh,
        in_specs=(
            P("space", ("groups", "snap")),
            P("space", None, None, None),
            P("space", None),
            P("space"),
            P(("groups", "snap"), None),
            P(),
        ),
        out_specs=P(("space", "snap"), "groups"),
        check_vma=False,
    )
```

```python
import functools

import jax
import jax.numpy as jnp
from jax import lax
from jax.experimental import pallas as pl
from jax.experimental.pallas import tpu as pltpu
from jax.sharding import PartitionSpec as P

HIGH = lax.Precision.HIGHEST
MESH = pl.DeviceIdType.MESH
F32 = jnp.float32
BF16 = jnp.bfloat16
VMEM = pl.BlockSpec(memory_space=pltpu.VMEM)
ROWS_IN_STEP = 8
LAG = 3
TN = (((0,), (0,)), ((), ()))
NT = (((1,), (1,)), ((), ()))


def dot(a, b, dims=(((1,), (0,)), ((), ())), precision=None):
    return lax.dot_general(a, b, dims, precision=precision, preferred_element_type=F32)


def upper_blocks(count):
    return [(i, j) for i in range(count) for j in range(i, count)]


def weigh_kernel(cols_ref, counts_ref, snaps_ref, blocks_ref, weighted_ref, tri_ref, gram):
    step = pl.program_id(0)
    in_step, slots, width, _ = blocks_ref.shape
    for i in range(in_step):
        row = step * in_step + i
        count = counts_ref[row]
        factors = []
        sources = []
        for slot in range(slots):
            factor = blocks_ref[i, slot]
            factors.append(jnp.where(slot < count, factor, jnp.zeros_like(factor)))
            start = pl.multiple_of(cols_ref[slot, row] * width, width)
            sources.append(snaps_ref[pl.ds(start, width), :])
        product = dot(jnp.concatenate(factors, axis=1), jnp.concatenate(sources, axis=0))
        weighted_ref[i * width : (i + 1) * width, :] = product.astype(BF16)
    size = gram.shape[0]
    tall = 256

    @pl.when(step == 0)
    def _():
        gram[...] = jnp.zeros_like(gram)

    for low in range(0, size, tall):
        gram[low : low + tall, low:] += dot(
            weighted_ref[:, low : low + tall], weighted_ref[:, low:], TN
        )

    @pl.when(step == pl.num_programs(0) - 1)
    def _():
        for index, (i, j) in enumerate(upper_blocks(size // 128)):
            tri_ref[index] = gram[i * 128 : (i + 1) * 128, j * 128 : (j + 1) * 128]


def weigh(snapshots, factor_blocks, factor_cols, factor_counts):
    rows, size = snapshots.shape
    row_blocks, slots, width, _ = factor_blocks.shape
    in_step = ROWS_IN_STEP
    count = len(upper_blocks(size // 128))
    return pl.pallas_call(
        weigh_kernel,
        grid=(row_blocks // in_step,),
        in_specs=[
            pl.BlockSpec(memory_space=pltpu.SMEM),
            pl.BlockSpec(memory_space=pltpu.SMEM),
            pl.BlockSpec((rows, size), lambda s: (0, 0)),
            pl.BlockSpec((in_step, slots, width, width), lambda s: (s, 0, 0, 0)),
        ],
        out_specs=[
            pl.BlockSpec((in_step * width, size), lambda s: (s, 0)),
            pl.BlockSpec((count, 128, 128), lambda s: (0, 0, 0)),
        ],
        out_shape=[
            jax.ShapeDtypeStruct((rows, size), BF16),
            jax.ShapeDtypeStruct((count, 128, 128), F32),
        ],
        scratch_shapes=[pltpu.VMEM((size, size), F32)],
        name="weigh",
    )(factor_cols.T, factor_counts, snapshots, factor_blocks)


def line_kernel(n, own, total, pre_in, pre_out, suf_in, suf_out, sems):
    me = lax.axis_index("space")
    has_left = me > 0
    has_right = me < n - 1
    barrier = pltpu.get_barrier_semaphore()

    @pl.when(has_left)
    def _():
        pl.semaphore_signal(barrier, inc=1, device_id={"space": me - 1}, device_id_type=MESH)

    @pl.when(has_right)
    def _():
        pl.semaphore_signal(barrier, inc=1, device_id={"space": me + 1}, device_id_type=MESH)

    pl.semaphore_wait(barrier, has_left.astype(jnp.int32) + has_right.astype(jnp.int32))

    chunks = own.shape[0]

    def copy(kind, c, other):
        source, target = ((pre_out, pre_in), (suf_out, suf_in))[kind]
        return pltpu.make_async_remote_copy(
            src_ref=source.at[c],
            dst_ref=target.at[c],
            send_sem=sems.at[2 * kind, c],
            recv_sem=sems.at[2 * kind + 1, c],
            device_id={"space": other},
            device_id_type=MESH,
        )

    def turn(t, carry):
        for kind, behind, has_from, has_to, to, out, arrived in (
            (0, me, has_left, has_right, me + 1, pre_out, pre_in),
            (1, n - 1 - me, has_right, has_left, me - 1, suf_out, suf_in),
        ):
            c = t - LAG * behind
            here = jnp.logical_and(c >= 0, c < chunks)

            @pl.when(jnp.logical_and(here, has_from))
            def _():
                copy(kind, c, me).wait_recv()

            @pl.when(jnp.logical_and(here, jnp.logical_and(has_to, has_from)))
            def _():
                out[c] = (own[c] + arrived[c].astype(F32)).astype(BF16)

            @pl.when(jnp.logical_and(here, jnp.logical_and(has_to, jnp.logical_not(has_from))))
            def _():
                out[c] = own[c].astype(BF16)

            @pl.when(jnp.logical_and(here, has_to))
            def _():
                copy(kind, c, to).start()

        return carry

    lax.fori_loop(0, chunks + LAG * (n - 1), turn, 0)

    for c in range(chunks):
        total[c] = own[c]

    @pl.when(has_left)
    def _():
        for c in range(chunks):
            total[c] += pre_in[c].astype(F32)

    @pl.when(has_right)
    def _():
        for c in range(chunks):
            total[c] += suf_in[c].astype(F32)

    for c in range(chunks):

        @pl.when(has_right)
        def _():
            copy(0, c, me).wait_send()

        @pl.when(has_left)
        def _():
            copy(1, c, me).wait_send()


def sum_over_space(blocks):
    n = lax.axis_size("space")
    return pl.pallas_call(
        functools.partial(line_kernel, n),
        in_specs=[VMEM],
        out_specs=VMEM,
        out_shape=jax.ShapeDtypeStruct(blocks.shape, F32),
        scratch_shapes=[pltpu.VMEM(blocks.shape, BF16)] * 4
        + [pltpu.SemaphoreType.DMA((4, blocks.shape[0]))],
        compiler_params=pltpu.CompilerParams(collective_id=0, has_side_effects=True),
        name="line_sum",
    )(blocks)


def eliminate(a, e, lane):
    a, e = list(a), list(e)
    groups = len(a)
    row = lax.broadcasted_iota(jnp.int32, (8, 128), 0)
    scale = [jnp.zeros((8, 128), F32)] * groups
    for g in range(groups):
        cols = {
            h: [
                jnp.broadcast_to(a[h][:, lane + 8 * g + k : lane + 8 * g + k + 1], (8, 128))
                for k in range(8)
            ]
            for h in range(g, groups)
        }
        for k in range(8):
            pivot = jnp.broadcast_to(cols[g][k][k : k + 1, :], (8, 128))
            inverse = 1.0 / pivot
            scale[g] = jnp.where(row == k, lax.rsqrt(pivot), scale[g])
            a_row = jnp.broadcast_to(a[g][k : k + 1, :], (8, 128))
            e_row = jnp.broadcast_to(e[g][k : k + 1, :], (8, 128))
            heads = {
                m: jnp.broadcast_to(cols[g][m][k : k + 1, :], (8, 128)) for m in range(k + 1, 8)
            }
            for h in range(g, groups):
                if h == g and k == 7:
                    continue
                f = cols[h][k] * inverse
                if h == g:
                    f = jnp.where(row > k, f, 0.0)
                for m in range(k + 1, 8):
                    cols[h][m] = cols[h][m] - f * heads[m]
                a[h] = a[h] - f * a_row
                e[h] = e[h] - f * e_row
    return [x * s for x, s in zip(a, scale)], [x * s for x, s in zip(e, scale)]


def inverse_factor(cross):
    size = cross.shape[0]
    row = lax.broadcasted_iota(jnp.int32, (size, size), 0)
    col = lax.broadcasted_iota(jnp.int32, (size, size), 1)
    both = jnp.concatenate([cross, (row == col).astype(F32)], axis=1)
    done = []
    for p in range(size // 32):
        rows = [both[p * 32 + 8 * g : p * 32 + 8 * g + 8] for g in range(4)]
        a, e = eliminate([r[:, :size] for r in rows], [r[:, size:] for r in rows], p * 32)
        a, e = jnp.concatenate(a, axis=0), jnp.concatenate(e, axis=0)
        done.append(e)
        if p < size // 32 - 1:
            both = both - dot(a, jnp.concatenate([a, e], axis=1), TN, HIGH)
    return jnp.concatenate(done, axis=0)


def orthonormal(z):
    return dot(z, inverse_factor(dot(z, z, TN, HIGH)), NT, HIGH)


def compress_kernel(tri_ref, start_ref, weighted_ref, panel_ref, diag_ref, gram, basis):
    size = gram.shape[0]
    for index, (i, j) in enumerate(upper_blocks(size // 128)):
        block = tri_ref[index]
        gram[i * 128 : (i + 1) * 128, j * 128 : (j + 1) * 128] = block
        if i != j:
            gram[j * 128 : (j + 1) * 128, i * 128 : (i + 1) * 128] = block.T
    basis[...] = start_ref[...]

    def sweep(_, carry):
        basis[...] = orthonormal(dot(gram[...], basis[...], precision=HIGH))
        return carry

    lax.fori_loop(0, 2, sweep, 0)
    rounded = basis[...].astype(BF16)
    tall = 1024
    for low in range(0, weighted_ref.shape[0], tall):
        panel_ref[low : low + tall, :] = dot(weighted_ref[low : low + tall, :], rounded).astype(BF16)
    wide = rounded.astype(F32)
    diag_ref[...] = dot(wide, dot(gram[...], wide, precision=HIGH), TN, HIGH)


def compress(tri, start_basis, weighted):
    size, modes = start_basis.shape
    return pl.pallas_call(
        compress_kernel,
        in_specs=[VMEM] * 3,
        out_specs=[VMEM] * 2,
        out_shape=[
            jax.ShapeDtypeStruct((weighted.shape[0], modes), BF16),
            jax.ShapeDtypeStruct((modes, modes), F32),
        ],
        scratch_shapes=[pltpu.VMEM((size, size), F32), pltpu.VMEM((size, modes), F32)],
        name="compress",
    )(tri, start_basis, weighted)


def flipped(index, bit):
    return index + (1 - 2 * (index // (1 << bit) % 2)) * (1 << bit)


def pair_kernel(
    n,
    level,
    panel,
    diag,
    pair,
    cross_gram,
    got,
    got_diag,
    mine_all,
    out,
    came,
    z_out,
    z_came,
    sum_out,
    sum_came,
    sems,
    x_sems,
    z_sems,
    s_sems,
):
    snap = lax.axis_index("snap")
    space = lax.axis_index("space")
    bit = snap // (1 << level) % 2
    partner = flipped(snap, level)
    half, _, rows, modes = panel.shape
    barrier = pltpu.get_barrier_semaphore()
    members = 1 << (level + 1)
    own = lax.rem(snap, members)
    share = modes // members

    def member(k):
        return snap - own + lax.rem(own + k, members)

    def share_of(k):
        return pl.ds(pl.multiple_of(lax.rem(own + k, members) * share, share), share)

    for k in range(1, members):
        pl.semaphore_signal(barrier, inc=1, device_id={"snap": member(k)}, device_id_type=MESH)
    for k in range(1, n):
        pl.semaphore_signal(
            barrier, inc=1, device_id={"space": lax.rem(space + k, n)}, device_id_type=MESH
        )
    pl.semaphore_wait(barrier, members - 1 + n - 1)

    def remote(source, target, send, recv, device):
        return pltpu.make_async_remote_copy(
            src_ref=source,
            dst_ref=target,
            send_sem=send,
            recv_sem=recv,
            device_id=device,
            device_id_type=MESH,
        )

    copies = [
        remote(panel.at[h, 1 - bit], got.at[h], sems.at[0, h], sems.at[1, h], {"snap": partner})
        for h in range(half)
    ]
    copies.append(
        remote(diag, got_diag, sems.at[0, half], sems.at[1, half], {"snap": partner})
    )
    for c in copies:
        c.start()
    cross = jnp.zeros((modes, modes), F32)
    upper = bit == 1
    for h in range(half):
        copies[h].wait_recv()
        mine, theirs = panel[h, bit], got[h]
        left = jnp.where(upper, theirs, mine)
        right = jnp.where(upper, mine, theirs)
        pair[h * rows : (h + 1) * rows, :modes] = left
        pair[h * rows : (h + 1) * rows, modes:] = right
        cross = cross + dot(left, right, TN)
    mine_all[...] = cross
    out[...] = cross.astype(BF16)
    spread = [
        remote(
            out.at[share_of(k)],
            came.at[k - 1],
            x_sems.at[0, k - 1],
            x_sems.at[1, k - 1],
            {"snap": member(k)},
        )
        for k in range(1, members)
    ]
    for c in spread:
        c.start()
    part = mine_all[share_of(0), :]
    for k, c in enumerate(spread):
        c.wait_recv()
        part = part + came[k].astype(F32)
    z_out[...] = part.astype(BF16)
    steps = [
        remote(
            z_out,
            z_came.at[k - 1],
            z_sems.at[0, k - 1],
            z_sems.at[1, k - 1],
            {"space": lax.rem(space + k, n)},
        )
        for k in range(1, n)
    ]
    for s in steps:
        s.start()
    copies[half].wait_recv()
    cross_gram[:modes, :modes] = jnp.where(upper, got_diag[...], diag[...])
    cross_gram[modes:, modes:] = jnp.where(upper, diag[...], got_diag[...])
    for k, s in enumerate(steps):
        s.wait_recv()
        part = part + z_came[k].astype(F32)
    sum_out[...] = part.astype(BF16)
    collected = [
        remote(
            sum_out,
            sum_came.at[k - 1],
            s_sems.at[0, k - 1],
            s_sems.at[1, k - 1],
            {"snap": member(k)},
        )
        for k in range(1, members)
    ]
    for c in collected:
        c.start()
    cross_gram[share_of(0), modes:] = part.astype(BF16).astype(F32)
    for k, c in enumerate(collected):
        c.wait_recv()
        cross_gram[share_of(members - 1 - k), modes:] = sum_came[k].astype(F32)
    cross = cross_gram[:modes, modes:]
    cross_gram[modes:, :modes] = cross.T
    for c in copies + spread + steps + collected:
        c.wait_send()


def pair_up(panel, diag, level, parts):
    n = lax.axis_size("space")
    rows, modes = panel.shape
    half = parts // 2
    rows_in = rows // parts
    members = 1 << (level + 1)
    share = modes // members
    return pl.pallas_call(
        functools.partial(pair_kernel, n, level),
        in_specs=[VMEM] * 2,
        out_specs=[VMEM] * 2,
        out_shape=[
            jax.ShapeDtypeStruct((rows // 2, 2 * modes), BF16),
            jax.ShapeDtypeStruct((2 * modes, 2 * modes), F32),
        ],
        scratch_shapes=[
            pltpu.VMEM((half, rows_in, modes), BF16),
            pltpu.VMEM((modes, modes), F32),
            pltpu.VMEM((modes, modes), F32),
            pltpu.VMEM((modes, modes), BF16),
            pltpu.VMEM((members - 1, share, modes), BF16),
            pltpu.VMEM((share, modes), BF16),
            pltpu.VMEM((n - 1, share, modes), BF16),
            pltpu.VMEM((share, modes), BF16),
            pltpu.VMEM((members - 1, share, modes), BF16),
            pltpu.SemaphoreType.DMA((2, half + 1)),
            pltpu.SemaphoreType.DMA((2, members - 1)),
            pltpu.SemaphoreType.DMA((2, n - 1)),
            pltpu.SemaphoreType.DMA((2, members - 1)),
        ],
        compiler_params=pltpu.CompilerParams(collective_id=1 + level, has_side_effects=True),
        name="pair_up",
    )(panel.reshape(half, 2, rows_in, modes), diag)


def mix_kernel(snap_count, level, pair, cross_gram, starts, *outs):
    snap = lax.axis_index("snap")
    index = snap_count - (snap_count >> level) + snap // (1 << (level + 1))
    steered = dot(cross_gram[...], starts[index], precision=HIGH)
    mixing = orthonormal(steered).astype(BF16)
    outs[0][...] = dot(pair[...], mixing).astype(BF16)
    if len(outs) > 1:
        wide = mixing.astype(F32)
        outs[1][...] = dot(wide, dot(cross_gram[...], wide, precision=HIGH), TN, HIGH)


def mix(pair, cross_gram, merge_starts, level, snap_count, last):
    rows = pair.shape[0]
    modes = merge_starts.shape[2]
    shapes = [jax.ShapeDtypeStruct((rows, modes), BF16)]
    if not last:
        shapes.append(jax.ShapeDtypeStruct((modes, modes), F32))
    return pl.pallas_call(
        functools.partial(mix_kernel, snap_count, level),
        in_specs=[VMEM] * 3,
        out_specs=[VMEM] * len(shapes),
        out_shape=shapes,
        name="mix",
    )(pair, cross_gram, merge_starts)


def local(snapshots, factor_blocks, factor_cols, factor_counts, start_basis, merge_starts):
    weighted, tri = weigh(snapshots, factor_blocks, factor_cols, factor_counts)
    tri = sum_over_space(tri)
    panel, diag = compress(tri, start_basis, weighted)
    parts = lax.axis_size("snap")
    snap_count = parts
    levels = snap_count.bit_length() - 1
    for level in range(levels):
        pair, cross_gram = pair_up(panel, diag, level, parts)
        parts //= 2
        last = level == levels - 1
        made = mix(pair, cross_gram, merge_starts, level, snap_count, last)
        panel = made[0]
        diag = None if last else made[1]
    return panel


def solution(mesh):
    return jax.shard_map(
        local,
        mesh=mesh,
        in_specs=(
            P("space", ("groups", "snap")),
            P("space", None, None, None),
            P("space", None),
            P("space"),
            P(("groups", "snap"), None),
            P(),
        ),
        out_specs=P(("space", "snap"), "groups"),
        check_vma=False,
    )
```

```python
import functools

import jax
import jax.numpy as jnp
from jax import lax
from jax.experimental import pallas as pl
from jax.experimental.pallas import tpu as pltpu
from jax.sharding import PartitionSpec as P

HIGH = lax.Precision.HIGHEST
MESH = pl.DeviceIdType.MESH
F32 = jnp.float32
BF16 = jnp.bfloat16
VMEM = pl.BlockSpec(memory_space=pltpu.VMEM)
ROWS_IN_STEP = 8
LAG = 3
TN = (((0,), (0,)), ((), ()))
NT = (((1,), (1,)), ((), ()))


def dot(a, b, dims=(((1,), (0,)), ((), ())), precision=None):
    return lax.dot_general(a, b, dims, precision=precision, preferred_element_type=F32)


def upper_blocks(count):
    return [(i, j) for i in range(count) for j in range(i, count)]


def weigh_kernel(cols_ref, counts_ref, snaps_ref, blocks_ref, weighted_ref, tri_ref, gram):
    step = pl.program_id(0)
    in_step, slots, width, _ = blocks_ref.shape
    for i in range(in_step):
        row = step * in_step + i
        count = counts_ref[row]
        factors = []
        sources = []
        for slot in range(slots):
            factor = blocks_ref[i, slot]
            factors.append(jnp.where(slot < count, factor, jnp.zeros_like(factor)))
            start = pl.multiple_of(cols_ref[slot, row] * width, width)
            sources.append(snaps_ref[pl.ds(start, width), :])
        product = dot(jnp.concatenate(factors, axis=1), jnp.concatenate(sources, axis=0))
        weighted_ref[i * width : (i + 1) * width, :] = product.astype(BF16)
    size = gram.shape[0]
    tall = 256

    @pl.when(step == 0)
    def _():
        gram[...] = jnp.zeros_like(gram)

    for low in range(0, size, tall):
        gram[low : low + tall, low:] += dot(
            weighted_ref[:, low : low + tall], weighted_ref[:, low:], TN
        )

    @pl.when(step == pl.num_programs(0) - 1)
    def _():
        for index, (i, j) in enumerate(upper_blocks(size // 128)):
            tri_ref[index] = gram[i * 128 : (i + 1) * 128, j * 128 : (j + 1) * 128]


def weigh(snapshots, factor_blocks, factor_cols, factor_counts):
    rows, size = snapshots.shape
    row_blocks, slots, width, _ = factor_blocks.shape
    in_step = ROWS_IN_STEP
    count = len(upper_blocks(size // 128))
    return pl.pallas_call(
        weigh_kernel,
        grid=(row_blocks // in_step,),
        in_specs=[
            pl.BlockSpec(memory_space=pltpu.SMEM),
            pl.BlockSpec(memory_space=pltpu.SMEM),
            pl.BlockSpec((rows, size), lambda s: (0, 0)),
            pl.BlockSpec((in_step, slots, width, width), lambda s: (s, 0, 0, 0)),
        ],
        out_specs=[
            pl.BlockSpec((in_step * width, size), lambda s: (s, 0)),
            pl.BlockSpec((count, 128, 128), lambda s: (0, 0, 0)),
        ],
        out_shape=[
            jax.ShapeDtypeStruct((rows, size), BF16),
            jax.ShapeDtypeStruct((count, 128, 128), F32),
        ],
        scratch_shapes=[pltpu.VMEM((size, size), F32)],
        name="weigh",
    )(factor_cols.T, factor_counts, snapshots, factor_blocks)


def line_sum(n, own, total, pre_in, pre_out, suf_in, suf_out, sems):
    me = lax.axis_index("space")
    has_left = me > 0
    has_right = me < n - 1
    chunks = own.shape[0]

    def copy(kind, c, other):
        source, target = ((pre_out, pre_in), (suf_out, suf_in))[kind]
        return pltpu.make_async_remote_copy(
            src_ref=source.at[c],
            dst_ref=target.at[c],
            send_sem=sems.at[2 * kind, c],
            recv_sem=sems.at[2 * kind + 1, c],
            device_id={"space": other},
            device_id_type=MESH,
        )

    def turn(t, carry):
        for kind, behind, has_from, has_to, to, out, arrived in (
            (0, me, has_left, has_right, me + 1, pre_out, pre_in),
            (1, n - 1 - me, has_right, has_left, me - 1, suf_out, suf_in),
        ):
            c = t - LAG * behind
            here = jnp.logical_and(c >= 0, c < chunks)

            @pl.when(jnp.logical_and(here, has_from))
            def _():
                copy(kind, c, me).wait_recv()

            @pl.when(jnp.logical_and(here, jnp.logical_and(has_to, has_from)))
            def _():
                out[c] = (own[c] + arrived[c].astype(F32)).astype(BF16)

            @pl.when(jnp.logical_and(here, jnp.logical_and(has_to, jnp.logical_not(has_from))))
            def _():
                out[c] = own[c].astype(BF16)

            @pl.when(jnp.logical_and(here, has_to))
            def _():
                copy(kind, c, to).start()

        return carry

    lax.fori_loop(0, chunks + LAG * (n - 1), turn, 0)

    for c in range(chunks):
        total[c] = own[c]

    @pl.when(has_left)
    def _():
        for c in range(chunks):
            total[c] += pre_in[c].astype(F32)

    @pl.when(has_right)
    def _():
        for c in range(chunks):
            total[c] += suf_in[c].astype(F32)

    for c in range(chunks):

        @pl.when(has_right)
        def _():
            copy(0, c, me).wait_send()

        @pl.when(has_left)
        def _():
            copy(1, c, me).wait_send()


def eliminate(a, e, lane):
    a, e = list(a), list(e)
    groups = len(a)
    row = lax.broadcasted_iota(jnp.int32, (8, 128), 0)
    scale = [jnp.zeros((8, 128), F32)] * groups
    for g in range(groups):
        cols = {
            h: [
                jnp.broadcast_to(a[h][:, lane + 8 * g + k : lane + 8 * g + k + 1], (8, 128))
                for k in range(8)
            ]
            for h in range(g, groups)
        }
        for k in range(8):
            pivot = jnp.broadcast_to(cols[g][k][k : k + 1, :], (8, 128))
            inverse = 1.0 / pivot
            scale[g] = jnp.where(row == k, lax.rsqrt(pivot), scale[g])
            a_row = jnp.broadcast_to(a[g][k : k + 1, :], (8, 128))
            e_row = jnp.broadcast_to(e[g][k : k + 1, :], (8, 128))
            heads = {
                m: jnp.broadcast_to(cols[g][m][k : k + 1, :], (8, 128)) for m in range(k + 1, 8)
            }
            for h in range(g, groups):
                if h == g and k == 7:
                    continue
                f = cols[h][k] * inverse
                if h == g:
                    f = jnp.where(row > k, f, 0.0)
                for m in range(k + 1, 8):
                    cols[h][m] = cols[h][m] - f * heads[m]
                a[h] = a[h] - f * a_row
                e[h] = e[h] - f * e_row
    return [x * s for x, s in zip(a, scale)], [x * s for x, s in zip(e, scale)]


def inverse_factor(cross):
    size = cross.shape[0]
    row = lax.broadcasted_iota(jnp.int32, (size, size), 0)
    col = lax.broadcasted_iota(jnp.int32, (size, size), 1)
    both = jnp.concatenate([cross, (row == col).astype(F32)], axis=1)
    done = []
    for p in range(size // 32):
        rows = [both[p * 32 + 8 * g : p * 32 + 8 * g + 8] for g in range(4)]
        a, e = eliminate([r[:, :size] for r in rows], [r[:, size:] for r in rows], p * 32)
        a, e = jnp.concatenate(a, axis=0), jnp.concatenate(e, axis=0)
        done.append(e)
        if p < size // 32 - 1:
            both = both - dot(a, jnp.concatenate([a, e], axis=1), TN, HIGH)
    return jnp.concatenate(done, axis=0)


def orthonormal(z):
    return dot(z, inverse_factor(dot(z, z, TN, HIGH)), NT, HIGH)


def compress(tri_ref, start_ref, gram, basis, diag_ref):
    size = gram.shape[0]
    for index, (i, j) in enumerate(upper_blocks(size // 128)):
        block = tri_ref[index]
        gram[i * 128 : (i + 1) * 128, j * 128 : (j + 1) * 128] = block
        if i != j:
            gram[j * 128 : (j + 1) * 128, i * 128 : (i + 1) * 128] = block.T
    basis[...] = start_ref[...]

    def sweep(_, carry):
        basis[...] = orthonormal(dot(gram[...], basis[...], precision=HIGH))
        return carry

    lax.fori_loop(0, 2, sweep, 0)
    rounded = basis[...].astype(BF16)
    wide = rounded.astype(F32)
    diag_ref[...] = dot(wide, dot(gram[...], wide, precision=HIGH), TN, HIGH)
    return rounded


def flipped(index, bit):
    return index + (1 - 2 * (index // (1 << bit) % 2)) * (1 << bit)


def remote(source, target, send, recv, device):
    return pltpu.make_async_remote_copy(
        src_ref=source,
        dst_ref=target,
        send_sem=send,
        recv_sem=recv,
        device_id=device,
        device_id_type=MESH,
    )


def pair_up(n, level, make, diag, panel, pair, cross_gram, scratch):
    (got, got_diag, mine_all, out, came, z_out, z_came, sum_out, sum_came) = scratch[:9]
    sems, x_sems, z_sems, s_sems = scratch[9:]
    snap = lax.axis_index("snap")
    space = lax.axis_index("space")
    bit = snap // (1 << level) % 2
    partner = flipped(snap, level)
    half, _, rows, modes = panel.shape
    members = 1 << (level + 1)
    own = lax.rem(snap, members)
    share = modes // members

    def member(k):
        return snap - own + lax.rem(own + k, members)

    def share_of(k):
        return pl.ds(pl.multiple_of(lax.rem(own + k, members) * share, share), share)

    copies = [
        remote(panel.at[h, 1 - bit], got.at[h], sems.at[0, h], sems.at[1, h], {"snap": partner})
        for h in range(half)
    ]
    copies.append(remote(diag, got_diag, sems.at[0, half], sems.at[1, half], {"snap": partner}))
    for h in range(half):
        panel[h, 1 - bit] = make(h, 1 - bit)
        copies[h].start()
    copies[half].start()
    for h in range(half):
        panel[h, bit] = make(h, bit)
    cross = jnp.zeros((modes, modes), F32)
    upper = bit == 1
    for h in range(half):
        copies[h].wait_recv()
        mine, theirs = panel[h, bit], got[h]
        left = jnp.where(upper, theirs, mine)
        right = jnp.where(upper, mine, theirs)
        pair[h * rows : (h + 1) * rows, :modes] = left
        pair[h * rows : (h + 1) * rows, modes:] = right
        cross = cross + dot(left, right, TN)
    mine_all[...] = cross
    out[...] = cross.astype(BF16)
    spread = [
        remote(
            out.at[share_of(k)],
            came.at[k - 1],
            x_sems.at[0, k - 1],
            x_sems.at[1, k - 1],
            {"snap": member(k)},
        )
        for k in range(1, members)
    ]
    for c in spread:
        c.start()
    part = mine_all[share_of(0), :]
    for k, c in enumerate(spread):
        c.wait_recv()
        part = part + came[k].astype(F32)
    z_out[...] = part.astype(BF16)
    steps = [
        remote(
            z_out,
            z_came.at[k - 1],
            z_sems.at[0, k - 1],
            z_sems.at[1, k - 1],
            {"space": lax.rem(space + k, n)},
        )
        for k in range(1, n)
    ]
    for s in steps:
        s.start()
    copies[half].wait_recv()
    cross_gram[:modes, :modes] = jnp.where(upper, got_diag[...], diag[...])
    cross_gram[modes:, modes:] = jnp.where(upper, diag[...], got_diag[...])
    for k, s in enumerate(steps):
        s.wait_recv()
        part = part + z_came[k].astype(F32)
    sum_out[...] = part.astype(BF16)
    collected = [
        remote(
            sum_out,
            sum_came.at[k - 1],
            s_sems.at[0, k - 1],
            s_sems.at[1, k - 1],
            {"snap": member(k)},
        )
        for k in range(1, members)
    ]
    for c in collected:
        c.start()
    cross_gram[share_of(0), modes:] = part.astype(BF16).astype(F32)
    for k, c in enumerate(collected):
        c.wait_recv()
        cross_gram[share_of(members - 1 - k), modes:] = sum_came[k].astype(F32)
    cross = cross_gram[:modes, modes:]
    cross_gram[modes:, :modes] = cross.T
    for c in copies + spread + steps + collected:
        c.wait_send()


def mixing_of(cross_gram, starts, level, snap_count):
    snap = lax.axis_index("snap")
    index = snap_count - (snap_count >> level) + snap // (1 << (level + 1))
    return orthonormal(dot(cross_gram[...], starts[index], precision=HIGH)).astype(BF16)


def pair_scratch(n, level, parts, rows_in, modes):
    half = parts // 2
    members = 1 << (level + 1)
    share = modes // members
    return [
        pltpu.VMEM((half, rows_in, modes), BF16),
        pltpu.VMEM((modes, modes), F32),
        pltpu.VMEM((modes, modes), F32),
        pltpu.VMEM((modes, modes), BF16),
        pltpu.VMEM((members - 1, share, modes), BF16),
        pltpu.VMEM((share, modes), BF16),
        pltpu.VMEM((n - 1, share, modes), BF16),
        pltpu.VMEM((share, modes), BF16),
        pltpu.VMEM((members - 1, share, modes), BF16),
        pltpu.SemaphoreType.DMA((2, half + 1)),
        pltpu.SemaphoreType.DMA((2, members - 1)),
        pltpu.SemaphoreType.DMA((2, n - 1)),
        pltpu.SemaphoreType.DMA((2, members - 1)),
        pltpu.VMEM((half, 2, rows_in, modes), BF16),
        pltpu.VMEM((modes, modes), F32),
        pltpu.VMEM((half * rows_in, 2 * modes), BF16),
        pltpu.VMEM((2 * modes, 2 * modes), F32),
    ]


PER_LEVEL = 17


def tree_kernel(n, snap_count, tri, start, weighted_in, starts, pair_out, gram_out, *scratch):
    line, (gram, basis, weighted, sem) = scratch[:6], scratch[6:10]
    snap = lax.axis_index("snap")
    space = lax.axis_index("space")
    load = pltpu.make_async_copy(weighted_in, weighted, sem)
    load.start()
    barrier = pltpu.get_barrier_semaphore()
    for k in range(1, snap_count):
        other = lax.rem(snap + k, snap_count)
        pl.semaphore_signal(barrier, inc=1, device_id={"snap": other}, device_id_type=MESH)
    for k in range(1, n):
        other = lax.rem(space + k, n)
        pl.semaphore_signal(barrier, inc=1, device_id={"space": other}, device_id_type=MESH)
    pl.semaphore_wait(barrier, snap_count - 1 + n - 1)

    line_sum(n, tri, *line)
    levels = snap_count.bit_length() - 1
    parts = snap_count
    for level in range(levels):
        own = scratch[10 + level * PER_LEVEL : 10 + (level + 1) * PER_LEVEL]
        panel, diag, pair, cross_gram = own[13:]
        rows = panel.shape[2]
        if level == 0:
            rounded = compress(line[0], start, gram, basis, diag)
            load.wait()

            def make(h, side):
                low = pl.multiple_of((2 * h + side) * rows, rows)
                return dot(weighted[pl.ds(low, rows), :], rounded).astype(BF16)
        else:
            mixing = mixing_of(below_gram, starts, level - 1, snap_count)
            wide = mixing.astype(F32)
            diag[...] = dot(wide, dot(below_gram[...], wide, precision=HIGH), TN, HIGH)

            def make(h, side):
                low = pl.multiple_of((2 * h + side) * rows, rows)
                return dot(below[pl.ds(low, rows), :], mixing).astype(BF16)

        if level == levels - 1:
            pair, cross_gram = pair_out, gram_out
        pair_up(n, level, make, diag, panel, pair, cross_gram, own[:13])
        below, below_gram = pair, cross_gram


def tree(tri, start_basis, weighted, merge_starts):
    n = lax.axis_size("space")
    snap_count = lax.axis_size("snap")
    size, modes = start_basis.shape
    rows_in = weighted.shape[0] // snap_count
    scratch = [pltpu.VMEM(tri.shape, F32)]
    scratch += [pltpu.VMEM(tri.shape, BF16)] * 4
    scratch += [pltpu.SemaphoreType.DMA((4, tri.shape[0]))]
    scratch += [
        pltpu.VMEM((size, size), F32),
        pltpu.VMEM((size, modes), F32),
        pltpu.VMEM(weighted.shape, BF16),
        pltpu.SemaphoreType.DMA,
    ]
    for level in range(snap_count.bit_length() - 1):
        scratch += pair_scratch(n, level, snap_count >> level, rows_in, modes)
    return pl.pallas_call(
        functools.partial(tree_kernel, n, snap_count),
        in_specs=[VMEM, VMEM, pl.BlockSpec(memory_space=pl.ANY), VMEM],
        out_specs=[VMEM] * 2,
        out_shape=[
            jax.ShapeDtypeStruct((rows_in, 2 * modes), BF16),
            jax.ShapeDtypeStruct((2 * modes, 2 * modes), F32),
        ],
        scratch_shapes=scratch,
        compiler_params=pltpu.CompilerParams(collective_id=0, has_side_effects=True),
        name="tree",
    )(tri, start_basis, weighted, merge_starts)


def mix_kernel(snap_count, pair, cross_gram, starts, modes_ref):
    level = snap_count.bit_length() - 2
    mixing = mixing_of(cross_gram, starts, level, snap_count)
    modes_ref[...] = dot(pair[...], mixing).astype(BF16)


def local(snapshots, factor_blocks, factor_cols, factor_counts, start_basis, merge_starts):
    weighted, tri = weigh(snapshots, factor_blocks, factor_cols, factor_counts)
    pair, cross_gram = tree(tri, start_basis, weighted, merge_starts)
    return pl.pallas_call(
        functools.partial(mix_kernel, lax.axis_size("snap")),
        in_specs=[VMEM] * 3,
        out_specs=VMEM,
        out_shape=jax.ShapeDtypeStruct((pair.shape[0], merge_starts.shape[2]), BF16),
        name="mix",
    )(pair, cross_gram, merge_starts)


def solution(mesh):
    return jax.shard_map(
        local,
        mesh=mesh,
        in_specs=(
            P("space", ("groups", "snap")),
            P("space", None, None, None),
            P("space", None),
            P("space"),
            P(("groups", "snap"), None),
            P(),
        ),
        out_specs=P(("space", "snap"), "groups"),
        check_vma=False,
    )
```

```python
import functools

import jax
import jax.numpy as jnp
from jax import lax
from jax.experimental import pallas as pl
from jax.experimental.pallas import tpu as pltpu
from jax.sharding import PartitionSpec as P

HIGH = lax.Precision.HIGHEST
MESH = pl.DeviceIdType.MESH
F32 = jnp.float32
BF16 = jnp.bfloat16
VMEM = pl.BlockSpec(memory_space=pltpu.VMEM)
ROWS_IN_STEP = 8
LAG = 3
TN = (((0,), (0,)), ((), ()))
NT = (((1,), (1,)), ((), ()))


def dot(a, b, dims=(((1,), (0,)), ((), ())), precision=None):
    return lax.dot_general(a, b, dims, precision=precision, preferred_element_type=F32)


def upper_blocks(count):
    return [(i, j) for i in range(count) for j in range(i, count)]


def weigh_kernel(cols_ref, counts_ref, snaps_ref, blocks_ref, weighted_ref, tri_ref, gram):
    step = pl.program_id(0)
    in_step, slots, width, _ = blocks_ref.shape
    for i in range(in_step):
        row = step * in_step + i
        count = counts_ref[row]
        factors = []
        sources = []
        for slot in range(slots):
            factor = blocks_ref[i, slot]
            factors.append(jnp.where(slot < count, factor, jnp.zeros_like(factor)))
            start = pl.multiple_of(cols_ref[slot, row] * width, width)
            sources.append(snaps_ref[pl.ds(start, width), :])
        product = dot(jnp.concatenate(factors, axis=1), jnp.concatenate(sources, axis=0))
        weighted_ref[i * width : (i + 1) * width, :] = product.astype(BF16)
    size = gram.shape[0]
    tall = 256

    @pl.when(step == 0)
    def _():
        gram[...] = jnp.zeros_like(gram)

    for low in range(0, size, tall):
        gram[low : low + tall, low:] += dot(
            weighted_ref[:, low : low + tall], weighted_ref[:, low:], TN
        )

    @pl.when(step == pl.num_programs(0) - 1)
    def _():
        for index, (i, j) in enumerate(upper_blocks(size // 128)):
            tri_ref[index] = gram[i * 128 : (i + 1) * 128, j * 128 : (j + 1) * 128]


def weigh(snapshots, factor_blocks, factor_cols, factor_counts):
    rows, size = snapshots.shape
    row_blocks, slots, width, _ = factor_blocks.shape
    in_step = ROWS_IN_STEP
    count = len(upper_blocks(size // 128))
    return pl.pallas_call(
        weigh_kernel,
        grid=(row_blocks // in_step,),
        in_specs=[
            pl.BlockSpec(memory_space=pltpu.SMEM),
            pl.BlockSpec(memory_space=pltpu.SMEM),
            pl.BlockSpec((rows, size), lambda s: (0, 0)),
            pl.BlockSpec((in_step, slots, width, width), lambda s: (s, 0, 0, 0)),
        ],
        out_specs=[
            pl.BlockSpec((in_step * width, size), lambda s: (s, 0)),
            pl.BlockSpec((count, 128, 128), lambda s: (0, 0, 0)),
        ],
        out_shape=[
            jax.ShapeDtypeStruct((rows, size), BF16),
            jax.ShapeDtypeStruct((count, 128, 128), F32),
        ],
        scratch_shapes=[pltpu.VMEM((size, size), F32)],
        name="weigh",
    )(factor_cols.T, factor_counts, snapshots, factor_blocks)


def line_sum(n, own, total, pre_in, pre_out, suf_in, suf_out, sems):
    me = lax.axis_index("space")
    has_left = me > 0
    has_right = me < n - 1
    chunks = own.shape[0]

    def copy(kind, c, other):
        source, target = ((pre_out, pre_in), (suf_out, suf_in))[kind]
        return pltpu.make_async_remote_copy(
            src_ref=source.at[c],
            dst_ref=target.at[c],
            send_sem=sems.at[2 * kind, c],
            recv_sem=sems.at[2 * kind + 1, c],
            device_id={"space": other},
            device_id_type=MESH,
        )

    def turn(t, carry):
        for kind, behind, has_from, has_to, to, out, arrived in (
            (0, me, has_left, has_right, me + 1, pre_out, pre_in),
            (1, n - 1 - me, has_right, has_left, me - 1, suf_out, suf_in),
        ):
            c = t - LAG * behind
            here = jnp.logical_and(c >= 0, c < chunks)

            @pl.when(jnp.logical_and(here, has_from))
            def _():
                copy(kind, c, me).wait_recv()

            @pl.when(jnp.logical_and(here, jnp.logical_and(has_to, has_from)))
            def _():
                out[c] = (own[c] + arrived[c].astype(F32)).astype(BF16)

            @pl.when(jnp.logical_and(here, jnp.logical_and(has_to, jnp.logical_not(has_from))))
            def _():
                out[c] = own[c].astype(BF16)

            @pl.when(jnp.logical_and(here, has_to))
            def _():
                copy(kind, c, to).start()

        return carry

    lax.fori_loop(0, chunks + LAG * (n - 1), turn, 0)

    for c in range(chunks):
        total[c] = own[c]

    @pl.when(has_left)
    def _():
        for c in range(chunks):
            total[c] += pre_in[c].astype(F32)

    @pl.when(has_right)
    def _():
        for c in range(chunks):
            total[c] += suf_in[c].astype(F32)

    for c in range(chunks):

        @pl.when(has_right)
        def _():
            copy(0, c, me).wait_send()

        @pl.when(has_left)
        def _():
            copy(1, c, me).wait_send()


def eliminate(a, e, lane):
    a, e = list(a), list(e)
    groups = len(a)
    row = lax.broadcasted_iota(jnp.int32, (8, 128), 0)
    scale = [jnp.zeros((8, 128), F32)] * groups
    for g in range(groups):
        cols = {
            h: [
                jnp.broadcast_to(a[h][:, lane + 8 * g + k : lane + 8 * g + k + 1], (8, 128))
                for k in range(8)
            ]
            for h in range(g, groups)
        }
        for k in range(8):
            pivot = jnp.broadcast_to(cols[g][k][k : k + 1, :], (8, 128))
            inverse = 1.0 / pivot
            scale[g] = jnp.where(row == k, lax.rsqrt(pivot), scale[g])
            a_row = jnp.broadcast_to(a[g][k : k + 1, :], (8, 128))
            e_row = jnp.broadcast_to(e[g][k : k + 1, :], (8, 128))
            heads = {
                m: jnp.broadcast_to(cols[g][m][k : k + 1, :], (8, 128)) for m in range(k + 1, 8)
            }
            for h in range(g, groups):
                if h == g and k == 7:
                    continue
                f = cols[h][k] * inverse
                if h == g:
                    f = jnp.where(row > k, f, 0.0)
                for m in range(k + 1, 8):
                    cols[h][m] = cols[h][m] - f * heads[m]
                a[h] = a[h] - f * a_row
                e[h] = e[h] - f * e_row
    return [x * s for x, s in zip(a, scale)], [x * s for x, s in zip(e, scale)]


def inverse_factor(cross):
    size = cross.shape[0]
    row = lax.broadcasted_iota(jnp.int32, (size, size), 0)
    col = lax.broadcasted_iota(jnp.int32, (size, size), 1)
    both = jnp.concatenate([cross, (row == col).astype(F32)], axis=1)
    done = []
    for p in range(size // 32):
        rows = [both[p * 32 + 8 * g : p * 32 + 8 * g + 8] for g in range(4)]
        a, e = eliminate([r[:, :size] for r in rows], [r[:, size:] for r in rows], p * 32)
        a, e = jnp.concatenate(a, axis=0), jnp.concatenate(e, axis=0)
        done.append(e)
        if p < size // 32 - 1:
            both = both - dot(a, jnp.concatenate([a, e], axis=1), TN, HIGH)
    return jnp.concatenate(done, axis=0)


def orthonormal(z):
    return dot(z, inverse_factor(dot(z, z, TN, HIGH)), NT, HIGH)


def compress(tri_ref, start_ref, gram, basis):
    size = gram.shape[0]
    for index, (i, j) in enumerate(upper_blocks(size // 128)):
        block = tri_ref[index]
        gram[i * 128 : (i + 1) * 128, j * 128 : (j + 1) * 128] = block
        if i != j:
            gram[j * 128 : (j + 1) * 128, i * 128 : (i + 1) * 128] = block.T
    basis[...] = start_ref[...]

    def sweep(_, carry):
        basis[...] = orthonormal(dot(gram[...], basis[...], precision=HIGH))
        return carry

    lax.fori_loop(0, 2, sweep, 0)
    return basis[...].astype(BF16)


def projected(cross, vectors):
    wide = vectors.astype(F32)
    return dot(wide, dot(cross[...], wide, precision=HIGH), TN, HIGH)


def flipped(index, bit):
    return index + (1 - 2 * (index // (1 << bit) % 2)) * (1 << bit)


def remote(source, target, send, recv, device):
    return pltpu.make_async_remote_copy(
        src_ref=source,
        dst_ref=target,
        send_sem=send,
        recv_sem=recv,
        device_id=device,
        device_id_type=MESH,
    )


def pair_up(n, level, make, make_diag, diag, panel, pair, cross_gram, scratch):
    (got, got_diag, mine_all, out, came, z_out, z_came, sum_out, sum_came) = scratch[:9]
    sems, x_sems, z_sems, s_sems = scratch[9:]
    snap = lax.axis_index("snap")
    space = lax.axis_index("space")
    bit = snap // (1 << level) % 2
    partner = flipped(snap, level)
    half, _, rows, modes = panel.shape
    members = 1 << (level + 1)
    own = lax.rem(snap, members)
    share = modes // members

    def member(k):
        return snap - own + lax.rem(own + k, members)

    def share_of(k):
        return pl.ds(pl.multiple_of(lax.rem(own + k, members) * share, share), share)

    copies = [
        remote(panel.at[h, 1 - bit], got.at[h], sems.at[0, h], sems.at[1, h], {"snap": partner})
        for h in range(half)
    ]
    copies.append(remote(diag, got_diag, sems.at[0, half], sems.at[1, half], {"snap": partner}))
    for h in range(half):
        panel[h, 1 - bit] = make(h, 1 - bit)
        copies[h].start()
    for h in range(half):
        panel[h, bit] = make(h, bit)
    diag[...] = make_diag()
    copies[half].start()
    cross = jnp.zeros((modes, modes), F32)
    upper = bit == 1
    for h in range(half):
        copies[h].wait_recv()
        mine, theirs = panel[h, bit], got[h]
        left = jnp.where(upper, theirs, mine)
        right = jnp.where(upper, mine, theirs)
        pair[h * rows : (h + 1) * rows, :modes] = left
        pair[h * rows : (h + 1) * rows, modes:] = right
        cross = cross + dot(left, right, TN)
    mine_all[...] = cross
    out[...] = cross.astype(BF16)
    spread = [
        remote(
            out.at[share_of(k)],
            came.at[k - 1],
            x_sems.at[0, k - 1],
            x_sems.at[1, k - 1],
            {"snap": member(k)},
        )
        for k in range(1, members)
    ]
    for c in spread:
        c.start()
    part = mine_all[share_of(0), :]
    for k, c in enumerate(spread):
        c.wait_recv()
        part = part + came[k].astype(F32)
    z_out[...] = part.astype(BF16)
    steps = [
        remote(
            z_out,
            z_came.at[k - 1],
            z_sems.at[0, k - 1],
            z_sems.at[1, k - 1],
            {"space": lax.rem(space + k, n)},
        )
        for k in range(1, n)
    ]
    for s in steps:
        s.start()
    copies[half].wait_recv()
    cross_gram[:modes, :modes] = jnp.where(upper, got_diag[...], diag[...])
    cross_gram[modes:, modes:] = jnp.where(upper, diag[...], got_diag[...])
    for k, s in enumerate(steps):
        s.wait_recv()
        part = part + z_came[k].astype(F32)
    sum_out[...] = part.astype(BF16)
    collected = [
        remote(
            sum_out,
            sum_came.at[k - 1],
            s_sems.at[0, k - 1],
            s_sems.at[1, k - 1],
            {"snap": member(k)},
        )
        for k in range(1, members)
    ]
    for c in collected:
        c.start()
    cross_gram[share_of(0), modes:] = part.astype(BF16).astype(F32)
    for k, c in enumerate(collected):
        c.wait_recv()
        cross_gram[share_of(members - 1 - k), modes:] = sum_came[k].astype(F32)
    cross = cross_gram[:modes, modes:]
    cross_gram[modes:, :modes] = cross.T
    for c in copies + spread + steps + collected:
        c.wait_send()


def mixing_of(cross_gram, starts, level, snap_count):
    snap = lax.axis_index("snap")
    index = snap_count - (snap_count >> level) + snap // (1 << (level + 1))
    return orthonormal(dot(cross_gram[...], starts[index], precision=HIGH)).astype(BF16)


def pair_scratch(n, level, parts, rows_in, modes):
    half = parts // 2
    members = 1 << (level + 1)
    share = modes // members
    return [
        pltpu.VMEM((half, rows_in, modes), BF16),
        pltpu.VMEM((modes, modes), F32),
        pltpu.VMEM((modes, modes), F32),
        pltpu.VMEM((modes, modes), BF16),
        pltpu.VMEM((members - 1, share, modes), BF16),
        pltpu.VMEM((share, modes), BF16),
        pltpu.VMEM((n - 1, share, modes), BF16),
        pltpu.VMEM((share, modes), BF16),
        pltpu.VMEM((members - 1, share, modes), BF16),
        pltpu.SemaphoreType.DMA((2, half + 1)),
        pltpu.SemaphoreType.DMA((2, members - 1)),
        pltpu.SemaphoreType.DMA((2, n - 1)),
        pltpu.SemaphoreType.DMA((2, members - 1)),
        pltpu.VMEM((half, 2, rows_in, modes), BF16),
        pltpu.VMEM((modes, modes), F32),
        pltpu.VMEM((half * rows_in, 2 * modes), BF16),
        pltpu.VMEM((2 * modes, 2 * modes), F32),
    ]


PER_LEVEL = 17


def tree_kernel(n, snap_count, tri, start, weighted_in, starts, pair_out, gram_out, *scratch):
    line, (gram, basis, weighted, sem) = scratch[:6], scratch[6:10]
    snap = lax.axis_index("snap")
    space = lax.axis_index("space")
    load = pltpu.make_async_copy(weighted_in, weighted, sem)
    load.start()
    barrier = pltpu.get_barrier_semaphore()
    for k in range(1, snap_count):
        other = lax.rem(snap + k, snap_count)
        pl.semaphore_signal(barrier, inc=1, device_id={"snap": other}, device_id_type=MESH)
    for k in range(1, n):
        other = lax.rem(space + k, n)
        pl.semaphore_signal(barrier, inc=1, device_id={"space": other}, device_id_type=MESH)
    pl.semaphore_wait(barrier, snap_count - 1 + n - 1)

    line_sum(n, tri, *line)
    levels = snap_count.bit_length() - 1
    parts = snap_count
    for level in range(levels):
        own = scratch[10 + level * PER_LEVEL : 10 + (level + 1) * PER_LEVEL]
        panel, diag, pair, cross_gram = own[13:]
        rows = panel.shape[2]
        if level == 0:
            rounded = compress(line[0], start, gram, basis)
            load.wait()

            def make(h, side):
                low = pl.multiple_of((2 * h + side) * rows, rows)
                return dot(weighted[pl.ds(low, rows), :], rounded).astype(BF16)

            def make_diag():
                return projected(gram, rounded)

        else:
            mixing = mixing_of(below_gram, starts, level - 1, snap_count)

            def make(h, side):
                low = pl.multiple_of((2 * h + side) * rows, rows)
                return dot(below[pl.ds(low, rows), :], mixing).astype(BF16)

            def make_diag():
                return projected(below_gram, mixing)

        if level == levels - 1:
            pair, cross_gram = pair_out, gram_out
        pair_up(n, level, make, make_diag, diag, panel, pair, cross_gram, own[:13])
        below, below_gram = pair, cross_gram


def tree(tri, start_basis, weighted, merge_starts):
    n = lax.axis_size("space")
    snap_count = lax.axis_size("snap")
    size, modes = start_basis.shape
    rows_in = weighted.shape[0] // snap_count
    scratch = [pltpu.VMEM(tri.shape, F32)]
    scratch += [pltpu.VMEM(tri.shape, BF16)] * 4
    scratch += [pltpu.SemaphoreType.DMA((4, tri.shape[0]))]
    scratch += [
        pltpu.VMEM((size, size), F32),
        pltpu.VMEM((size, modes), F32),
        pltpu.VMEM(weighted.shape, BF16),
        pltpu.SemaphoreType.DMA,
    ]
    for level in range(snap_count.bit_length() - 1):
        scratch += pair_scratch(n, level, snap_count >> level, rows_in, modes)
    return pl.pallas_call(
        functools.partial(tree_kernel, n, snap_count),
        in_specs=[VMEM, VMEM, pl.BlockSpec(memory_space=pl.ANY), VMEM],
        out_specs=[VMEM] * 2,
        out_shape=[
            jax.ShapeDtypeStruct((rows_in, 2 * modes), BF16),
            jax.ShapeDtypeStruct((2 * modes, 2 * modes), F32),
        ],
        scratch_shapes=scratch,
        compiler_params=pltpu.CompilerParams(collective_id=0, has_side_effects=True),
        name="tree",
    )(tri, start_basis, weighted, merge_starts)


def mix_kernel(snap_count, pair, cross_gram, starts, modes_ref):
    level = snap_count.bit_length() - 2
    mixing = mixing_of(cross_gram, starts, level, snap_count)
    modes_ref[...] = dot(pair[...], mixing).astype(BF16)


def local(snapshots, factor_blocks, factor_cols, factor_counts, start_basis, merge_starts):
    weighted, tri = weigh(snapshots, factor_blocks, factor_cols, factor_counts)
    pair, cross_gram = tree(tri, start_basis, weighted, merge_starts)
    return pl.pallas_call(
        functools.partial(mix_kernel, lax.axis_size("snap")),
        in_specs=[VMEM] * 3,
        out_specs=VMEM,
        out_shape=jax.ShapeDtypeStruct((pair.shape[0], merge_starts.shape[2]), BF16),
        name="mix",
    )(pair, cross_gram, merge_starts)


def solution(mesh):
    return jax.shard_map(
        local,
        mesh=mesh,
        in_specs=(
            P("space", ("groups", "snap")),
            P("space", None, None, None),
            P("space", None),
            P("space"),
            P(("groups", "snap"), None),
            P(),
        ),
        out_specs=P(("space", "snap"), "groups"),
        check_vma=False,
    )
```
